32 devices in a mesh: section: 4 (over y, x), dp: 8 (over z, core).
Axes of the slice: x: 2, y: 2, z: 4, core: 2. Of those that a mesh axis runs over, the one named last changes fastest.
Arguments:
- x_first: bfloat16 [4, 512, 4096], P('section', 'dp'), may hold values from -6 to 6
- x_second: bfloat16 [4, 512, 4096], P('section', 'dp'), may hold values from -6 to 6
- grad_first: bfloat16 [4, 512, 4096], P('section', 'dp'), may hold values from -6 to 6
- value_tiles: bfloat16 [4, 4, 16, 128, 128], P('section'), may hold values from -0.09375 to 0.09375
- output_tiles: bfloat16 [4, 4, 16, 128, 128], P('section'), may hold values from -0.125 to 0.125
- value_keep: int32 [4, 4, 16], P('section'), may hold values from 0 to 31, as said below
- output_keep: int32 [4, 4, 16], P('section'), may hold values from 0 to 31, as said below
Outputs:
- second_grad_in: bfloat16 [4, 512, 4096], P('section', 'dp')
- output_weight_grad: float32 [4, 64, 128, 128], P('section', 'dp')
The draws below stay inside these ranges and needn't reach their ends.
Inputs may be any that keep to these rules, and one draw needn't show every extreme that they name: `value_keep`: each row [s, c] lists 16 distinct feature blocks in increasing order. `output_keep`: each row [s, c] lists 16 distinct feature blocks in increasing order.
All inputs are finite; a program needn't handle non-finite values.
Results may differ from the reference program's by a relative error of at most 0.005.
Values may be sent and summed in bfloat16 or wider, within the bound.
No kernel may reach another device: no remote copies, remote signals or barrier semaphores. Data moves between devices by JAX's collectives and lax.ppermute only.
A program may use at most 64 MiB of HBM per device.

```python
import jax
import jax.numpy as jnp
from jax import lax

D = 4096
KV = 512
BLOCK = 128
SECTIONS = 4
REPLICAS = 8
TOKENS = 512
KVB = 4
KEEP = 16
TILES = 64


def keep_common(key, salt):
    row_count = SECTIONS * (KV // BLOCK)
    feat_blocks = D // BLOCK
    kept_count = D // BLOCK // 2
    row_keys = jax.random.split(jax.random.fold_in(key, salt), row_count)

    def permute_row(row_key):
        return jax.random.permutation(row_key, feat_blocks)
    shuffled = jax.vmap(permute_row)(row_keys)
    chosen = jnp.sort(shuffled[:, :kept_count], axis=1)
    return chosen.reshape(SECTIONS, KV // BLOCK, kept_count).astype(jnp.int32)


def draw_value_keep(key, part):
    return keep_common(key, 11)


def draw_output_keep(key, part):
    return keep_common(key, 23)


def spiked(values, key, source, target, parts, factor):
    owner, partner = [(jnp.arange(values.shape[position]) // (values.shape[position] // parts)).reshape([-1 if axis == position else 1 for axis in range(values.ndim)]) for position in (source, target)]
    chosen = jax.random.permutation(key, parts)[partner]
    strong = (owner == chosen) | (owner == (partner + parts // 2) % parts)
    return jnp.where(strong, factor * values, values)


def shard_levels(stream_key, extent, cuts, least, top_value):
    factor_of = 1.0
    for position, parts in cuts:
        steps = jax.random.uniform(jax.random.fold_in(jax.random.fold_in(stream_key, 6), position), (parts,), jnp.float32, least / len(cuts), top_value / len(cuts))
        factor_of = factor_of * jnp.repeat(jnp.exp(steps), extent[position] // parts).reshape((-1,) + (1,) * (len(extent) - 1 - position))
    return factor_of


def bell_draw(own_key, extent, deviation, most, shards=(), kind=jnp.bfloat16):
    result = deviation * jax.random.normal(own_key, extent, jnp.float32)
    if shards:
        result = result * shard_levels(own_key, extent, shards, -0.22, 0.18)
    return jnp.clip(result, -most, most).astype(kind)


def gaussian_with(stream_key, extent, scale, bound, cuts, heavy, kind=jnp.bfloat16):
    array = scale * jax.random.normal(stream_key, extent, jnp.float32)
    if cuts:
        array = array * shard_levels(stream_key, extent, cuts, -0.22, 0.18)
    return jnp.clip(spiked(array, jax.random.fold_in(stream_key, 3), *heavy), -bound, bound).astype(kind)


def setup_inputs(seed: int = 0) -> dict:
    splits = jax.random.split(jax.random.key(seed), 8)
    x_first = bell_draw(splits[0], (SECTIONS, TOKENS, D), 1.0, 6.0, ((0, 4), (1, 8)))
    x_second = bell_draw(splits[1], (SECTIONS, TOKENS, D), 1.0, 6.0, ((0, 4), (1, 8)))
    grad_first = gaussian_with(splits[2], (SECTIONS, TOKENS, D), 1.0, 6.0, ((0, 4), (1, 8)), (1, 2, 8, 2.0))
    value_tiles = bell_draw(splits[3], (SECTIONS, KVB, KEEP, BLOCK, BLOCK), D ** -0.5, 0.09375, ((0, 4),))
    output_tiles = bell_draw(splits[4], (SECTIONS, KVB, KEEP, BLOCK, BLOCK), (KEEP * BLOCK) ** -0.5, 0.125, ((0, 4),))
    value_keep = draw_value_keep(jax.random.fold_in(splits[7], 71), 0)
    output_keep = draw_output_keep(jax.random.fold_in(splits[7], 71), 0)
    return dict(x_first=x_first, x_second=x_second, grad_first=grad_first, value_tiles=value_tiles, output_tiles=output_tiles, value_keep=value_keep, output_keep=output_keep)


def layer_back(layer_in, upstream, w_value, w_output, value_idx, output_idx):
    tok_count = layer_in.shape[0]
    feat_blocks = layer_in.shape[1] // BLOCK
    gathered_in = layer_in.reshape(tok_count, feat_blocks, BLOCK)[:, value_idx]
    hidden_val = jnp.einsum('tcjb,cjbk->tck', gathered_in.astype(jnp.float32), w_value.astype(jnp.float32)).astype(jnp.bfloat16)
    up_blocks = upstream.reshape(tok_count, feat_blocks, BLOCK)
    gathered_up = up_blocks[:, output_idx]
    hidden_grad = jnp.einsum('tcjd,cjkd->tck', gathered_up.astype(jnp.float32), w_output.astype(jnp.float32)).astype(jnp.bfloat16)
    tile_grad = jnp.einsum('tck,tcjd->cjkd', hidden_val.astype(jnp.float32), gathered_up.astype(jnp.float32))
    partial_add = jnp.einsum('tck,cjbk->tcjb', hidden_grad.astype(jnp.float32), w_value.astype(jnp.float32))
    summed = up_blocks.astype(jnp.float32).at[:, value_idx].add(partial_add)
    return summed.reshape(tok_count, -1).astype(jnp.bfloat16), tile_grad


def section_step(packed):
    return layer_back(packed[0], packed[1], packed[2], packed[3], packed[4], packed[5])


def reference(x_first, x_second, grad_first, value_tiles, output_tiles, value_keep, output_keep):
    first_in, first_tiles = lax.map(section_step, (x_first, grad_first, value_tiles, output_tiles, value_keep, output_keep))
    arrived = jnp.roll(first_in, -1, axis=0)
    second_in, second_tiles = lax.map(section_step, (x_second, arrived, value_tiles, output_tiles, value_keep, output_keep))
    weight_grad = ((first_tiles + second_tiles) / (2.0 * REPLICAS)).reshape(SECTIONS, TILES, BLOCK, BLOCK)
    return second_in, weight_grad
```

```python
import functools

import jax
import jax.numpy as jnp
from jax import lax
from jax.experimental import pallas as pl
from jax.experimental.pallas import tpu as pltpu
from jax.sharding import PartitionSpec as P

F32 = jnp.float32
BF16 = jnp.bfloat16
NT = (((1,), (1,)), ((), ()))
NN = (((1,), (0,)), ((), ()))
VMEM = pl.BlockSpec(memory_space=pltpu.VMEM)
SMEM = pl.BlockSpec(memory_space=pltpu.SMEM)
HBM = pl.BlockSpec(memory_space=pl.ANY)


def block(ref, index, size):
    return ref[:, pl.ds(pl.multiple_of(index * size, size), size)]


def grad_kernel(parts_in, vk, ok, *refs):
    g_hbm = refs[:parts_in]
    o_hbm, v_hbm = refs[parts_in:parts_in + 2]
    outs = refs[parts_in + 2:-6]
    g_buf, o_buf, v_buf, acc, g_sem, w_sem = refs[-6:]
    kvb, keep, size, _ = o_buf.shape
    copies = []
    at = 0
    for i, part in enumerate(g_hbm):
        wide = part.shape[1]
        copies.append(pltpu.make_async_copy(part, g_buf.at[:, pl.ds(at, wide)], g_sem.at[i]))
        at += wide
    o_copies = [pltpu.make_async_copy(o_hbm.at[c], o_buf.at[c], w_sem.at[0, c]) for c in range(kvb)]
    v_copies = [pltpu.make_async_copy(v_hbm.at[c], v_buf.at[c], w_sem.at[1, c]) for c in range(kvb)]
    for copy in copies + o_copies + v_copies:
        copy.start()
    for copy in copies:
        copy.wait()
    hidden = []
    for c in range(kvb):
        o_copies[c].wait()
        total = None
        for j in range(0, keep, 2):
            left = jnp.concatenate([block(g_buf, ok[c, j + i], size) for i in (0, 1)], axis=1)
            right = jnp.concatenate([o_buf[c, j + i] for i in (0, 1)], axis=1)
            term = lax.dot_general(left, right, NT, preferred_element_type=F32)
            total = term if total is None else total + term
        hidden.append(total.astype(BF16))
    acc[...] = g_buf[...].astype(F32)
    for c in range(kvb):
        v_copies[c].wait()
        for j in range(keep):
            term = lax.dot_general(hidden[c], v_buf[c, j], NT, preferred_element_type=F32)
            cols = pl.ds(pl.multiple_of(vk[c, j] * size, size), size)
            acc[:, cols] = acc[:, cols] + term
    at = 0
    for out in outs:
        wide = out.shape[1]
        out[...] = acc[:, at:at + wide].astype(BF16)
        at += wide


def grad_call(g_parts, w_value, w_output, value_idx, output_idx, widths):
    tokens = g_parts[0].shape[0]
    width = sum(p.shape[1] for p in g_parts)
    kvb, keep, size, _ = w_value.shape
    flops = 4 * tokens * kvb * keep * size * size
    return pl.pallas_call(
        functools.partial(grad_kernel, len(g_parts)),
        out_shape=[jax.ShapeDtypeStruct((tokens, w), BF16) for w in widths],
        in_specs=[SMEM, SMEM] + [HBM] * (len(g_parts) + 2),
        out_specs=[VMEM] * len(widths),
        scratch_shapes=[
            pltpu.VMEM((tokens, width), BF16),
            pltpu.VMEM(w_output.shape, BF16),
            pltpu.VMEM(w_value.shape, BF16),
            pltpu.VMEM((tokens, width), F32),
            pltpu.SemaphoreType.DMA((len(g_parts),)),
            pltpu.SemaphoreType.DMA((2, kvb)),
        ],
        cost_estimate=pl.CostEstimate(flops=flops, bytes_accessed=6 << 20, transcendentals=0),
        name="grad",
    )(value_idx, output_idx, *g_parts, w_output, w_value)


def hidden_kernel(vk, x1_hbm, x2_hbm, v_hbm, out, x_buf, v_buf, x_sem, v_sem):
    tokens = x1_hbm.shape[0]
    kvb, keep, size, _ = v_buf.shape
    x_copies = [
        pltpu.make_async_copy(x1_hbm, x_buf.at[pl.ds(0, tokens)], x_sem.at[0]),
        pltpu.make_async_copy(x2_hbm, x_buf.at[pl.ds(tokens, tokens)], x_sem.at[1]),
    ]
    v_copies = [pltpu.make_async_copy(v_hbm.at[c], v_buf.at[c], v_sem.at[c]) for c in range(kvb)]
    for copy in x_copies + v_copies:
        copy.start()
    for copy in x_copies:
        copy.wait()
    for c in range(kvb):
        v_copies[c].wait()
        total = None
        for j in range(0, keep, 2):
            left = jnp.concatenate([block(x_buf, vk[c, j + i], size) for i in (0, 1)], axis=1)
            right = jnp.concatenate([v_buf[c, j + i] for i in (0, 1)], axis=0)
            term = lax.dot_general(left, right, NN, preferred_element_type=F32)
            total = term if total is None else total + term
        out[c] = total.astype(BF16).T


def hidden_call(x1, x2, w_value, value_idx):
    tokens, width = x1.shape
    kvb, keep, size, _ = w_value.shape
    return pl.pallas_call(
        hidden_kernel,
        out_shape=jax.ShapeDtypeStruct((kvb, size, 2 * tokens), BF16),
        in_specs=[SMEM, HBM, HBM, HBM],
        out_specs=VMEM,
        scratch_shapes=[
            pltpu.VMEM((2 * tokens, width), BF16),
            pltpu.VMEM(w_value.shape, BF16),
            pltpu.SemaphoreType.DMA((2,)),
            pltpu.SemaphoreType.DMA((kvb,)),
        ],
        cost_estimate=pl.CostEstimate(
            flops=4 * tokens * kvb * keep * size * size, bytes_accessed=4 << 20, transcendentals=0
        ),
        name="hidden",
    )(value_idx, x1, x2, w_value)


def reverse_bits(value, bits):
    out = 0
    for _ in range(bits):
        out, value = out * 2 + value % 2, value // 2
    return out


def tile_kernel(per, bits, me, ok, h_ref, g_ref, *refs):
    arrived, outs, stack = refs[:-5], refs[-5:-1], refs[-1]
    tokens = g_ref.shape[0]
    size = h_ref.shape[1]
    keep = ok.shape[1]
    stack[:tokens] = g_ref[...]
    at = 0
    for part in arrived:
        wide = part.shape[1]
        stack[tokens:, at:at + wide] = part[...]
        at += wide
    flip = me[0] * per
    position = (2 ** bits) * per - 1
    for out in outs:
        for i in reversed(range(out.shape[0])):
            tile = (reverse_bits(position // per, bits) * per + position % per) ^ flip
            c, j = tile // keep, lax.rem(tile, keep)
            term = lax.dot_general(
                h_ref[c], block(stack, ok[c, j], size), NN, preferred_element_type=F32
            )
            out[i] = term.astype(out.dtype)
            position -= 1


def tile_call(me, output_idx, hidden, g, arrived, ranks):
    kvb, size, stacked = hidden.shape
    keep = output_idx.shape[1]
    total = kvb * keep
    bits = ranks.bit_length() - 1
    per = total // ranks
    sizes = [(total // 4, BF16), (total // 4, BF16), (total // 4, F32), (total // 4, F32)]
    return pl.pallas_call(
        functools.partial(tile_kernel, per, bits),
        out_shape=[jax.ShapeDtypeStruct((n, size, size), t) for n, t in sizes],
        in_specs=[SMEM, SMEM] + [VMEM] * (2 + len(arrived)),
        out_specs=[VMEM] * 4,
        scratch_shapes=[pltpu.VMEM((stacked, g.shape[1]), BF16)],
        cost_estimate=pl.CostEstimate(
            flops=2 * stacked * total * size * size, bytes_accessed=4 << 20, transcendentals=0
        ),
        name="tiles",
    )(me, output_idx, hidden, g, *arrived)


def exchange(value, axis, bit):
    count = lax.axis_size(axis)
    return lax.ppermute(value, axis, [(i, i ^ bit) for i in range(count)])


def from_behind(value, axis, steps):
    count = lax.axis_size(axis)
    return lax.ppermute(value, axis, [(i, (i + steps) % count) for i in range(count)])


def per_device(x_first, x_second, grad_first, value_tiles, output_tiles, value_keep, output_keep):
    w_value, w_output = value_tiles[0], output_tiles[0]
    value_idx, output_idx = value_keep[0], output_keep[0]
    g = grad_first[0]
    width = g.shape[1]
    ranks = lax.axis_size("dp")
    me = lax.axis_index("dp").astype(jnp.int32).reshape(1)
    parts = 4
    widths = [width // parts] * parts
    first = grad_call([g], w_value, w_output, value_idx, output_idx, widths)
    arrived = [from_behind(p, "section", -1) for p in first]
    hidden = hidden_call(x_first[0], x_second[0], w_value, value_idx)
    send_near, send_far, keep_far, keep_near = tile_call(me, output_idx, hidden, g, arrived, ranks)
    got_near = exchange(send_near, "dp", 1)
    got_far = exchange(send_far, "dp", 1)
    (second,) = grad_call(arrived, w_value, w_output, value_idx, output_idx, [width])
    leaving = keep_far + got_near.astype(F32)
    staying = keep_near + got_far.astype(F32)
    bit = 2
    while bit < ranks:
        came = exchange(leaving.astype(BF16), "dp", bit).astype(F32)
        bit *= 2
        staying = staying + came
        half = staying.shape[0] // 2
        if bit < ranks:
            staying, leaving = staying[:half], staying[half:]
    weight_grad = staying * (1.0 / (2.0 * ranks))
    return second[None], weight_grad[None]


def solution(mesh):
    in_specs = (
        P("section", "dp", None),
        P("section", "dp", None),
        P("section", "dp", None),
        P("section", None, None, None, None),
        P("section", None, None, None, None),
        P("section", None, None),
        P("section", None, None),
    )
    out_specs = (P("section", "dp", None), P("section", "dp", None, None))
    return jax.shard_map(
        per_device, mesh=mesh, in_specs=in_specs, out_specs=out_specs, check_vma=False
    )
```

```python
import functools

import jax
import jax.numpy as jnp
from jax import lax
from jax.experimental import pallas as pl
from jax.experimental.pallas import tpu as pltpu
from jax.sharding import PartitionSpec as P

F32 = jnp.float32
BF16 = jnp.bfloat16
NT = (((1,), (1,)), ((), ()))
NN = (((1,), (0,)), ((), ()))
VMEM = pl.BlockSpec(memory_space=pltpu.VMEM)
SMEM = pl.BlockSpec(memory_space=pltpu.SMEM)
HBM = pl.BlockSpec(memory_space=pl.ANY)
ROOM = pltpu.CompilerParams(vmem_limit_bytes=16 << 20)


def cost(flops, nbytes):
    return pl.CostEstimate(flops=flops, bytes_accessed=nbytes, transcendentals=0)


def block(ref, index, size):
    return ref[:, pl.ds(pl.multiple_of(index * size, size), size)]


def pairs(keep):
    return [(j, j + 1) for j in range(0, keep, 2)]


def hidden_grad(ok, g, o, c):
    keep, size = o.shape[1], o.shape[2]
    total = None
    for both in pairs(keep):
        left = jnp.concatenate([block(g, ok[c, j], size) for j in both], axis=1)
        right = jnp.concatenate([o[c, j] for j in both], axis=1)
        term = lax.dot_general(left, right, NT, preferred_element_type=F32)
        total = term if total is None else total + term
    return total.astype(BF16)


def add_back(vk, hidden, v, c, acc):
    keep, size = v.shape[1], v.shape[2]
    for both in pairs(keep):
        right = jnp.concatenate([v[c, j] for j in both], axis=0)
        term = lax.dot_general(hidden, right, NT, preferred_element_type=F32)
        for i, j in enumerate(both):
            cols = pl.ds(pl.multiple_of(vk[c, j] * size, size), size)
            acc[:, cols] = acc[:, cols] + term[:, i * size:(i + 1) * size]


def write_parts(acc, outs):
    at = 0
    for out in outs:
        wide = out.shape[1]
        out[...] = acc[:, at:at + wide].astype(BF16)
        at += wide


def first_kernel(vk_hbm, ok_hbm, g_hbm, o_hbm, v_hbm, *refs):
    outs, (g, o, v, acc, vk, ok, sem, w_sem) = refs[:-8], refs[-8:]
    kvb = o.shape[0]
    copy = pltpu.make_async_copy
    small = [copy(ok_hbm, ok, sem.at[0]), copy(g_hbm, g, sem.at[1]), copy(vk_hbm, vk, sem.at[2])]
    o_copies = [copy(o_hbm.at[c], o.at[c], w_sem.at[0, c]) for c in range(kvb)]
    v_copies = [copy(v_hbm.at[c], v.at[c], w_sem.at[1, c]) for c in range(kvb)]
    for each in small + o_copies + v_copies:
        each.start()
    small[0].wait()
    small[1].wait()
    acc[...] = g[...].astype(F32)
    hidden = []
    for c in range(kvb):
        o_copies[c].wait()
        hidden.append(hidden_grad(ok, g, o, c))
    small[2].wait()
    for c in range(kvb):
        v_copies[c].wait()
        add_back(vk, hidden[c], v, c, acc)
    write_parts(acc, outs)


def first_call(g, w_value, w_output, value_idx, output_idx, widths):
    tokens, width = g.shape
    kvb, keep, size, _ = w_value.shape
    return pl.pallas_call(
        first_kernel,
        out_shape=[pltpu.VMEM((tokens, w), BF16) for w in widths],
        in_specs=[HBM] * 5,
        out_specs=[VMEM] * len(widths),
        scratch_shapes=[
            pltpu.VMEM((tokens, width), BF16),
            pltpu.VMEM(w_output.shape, BF16),
            pltpu.VMEM(w_value.shape, BF16),
            pltpu.VMEM((tokens, width), F32),
            pltpu.SMEM(value_idx.shape, jnp.int32),
            pltpu.SMEM(output_idx.shape, jnp.int32),
            pltpu.SemaphoreType.DMA((3,)),
            pltpu.SemaphoreType.DMA((2, kvb)),
        ],
        cost_estimate=cost(4 * tokens * kvb * keep * size * size, 5 << 20),
        name="first",
    )(value_idx, output_idx, g, w_output, w_value)


def second_kernel(vk, ok, o, v, *refs):
    arrived, (out, g, acc) = refs[:-3], refs[-3:]
    at = 0
    for part in arrived:
        wide = part.shape[1]
        g[:, at:at + wide] = part[...]
        acc[:, at:at + wide] = part[...].astype(F32)
        at += wide
    for c in range(o.shape[0]):
        add_back(vk, hidden_grad(ok, g, o, c), v, c, acc)
    write_parts(acc, [out])


def second_call(arrived, w_value, w_output, value_idx, output_idx):
    tokens = arrived[0].shape[0]
    width = sum(part.shape[1] for part in arrived)
    kvb, keep, size, _ = w_value.shape
    return pl.pallas_call(
        second_kernel,
        out_shape=jax.ShapeDtypeStruct((tokens, width), BF16),
        in_specs=[SMEM, SMEM] + [VMEM] * (2 + len(arrived)),
        out_specs=VMEM,
        scratch_shapes=[pltpu.VMEM((tokens, width), BF16), pltpu.VMEM((tokens, width), F32)],
        compiler_params=ROOM,
        cost_estimate=cost(4 * tokens * kvb * keep * size * size, 5 << 20),
        name="second",
    )(value_idx, output_idx, w_output, w_value, *arrived)


def hidden_kernel(vk, x1, x2, v, out, x):
    tokens = x1.shape[0]
    kvb, keep, size, _ = v.shape
    x[:tokens] = x1[...]
    x[tokens:] = x2[...]
    for c in range(kvb):
        total = None
        for both in pairs(keep):
            left = jnp.concatenate([block(x, vk[c, j], size) for j in both], axis=1)
            right = jnp.concatenate([v[c, j] for j in both], axis=0)
            term = lax.dot_general(left, right, NN, preferred_element_type=F32)
            total = term if total is None else total + term
        out[c] = total.astype(BF16).T


def hidden_call(x1, x2, w_value, value_idx):
    tokens, width = x1.shape
    kvb, keep, size, _ = w_value.shape
    return pl.pallas_call(
        hidden_kernel,
        out_shape=pltpu.VMEM((kvb, size, 2 * tokens), BF16),
        in_specs=[SMEM, VMEM, VMEM, VMEM],
        out_specs=VMEM,
        scratch_shapes=[pltpu.VMEM((2 * tokens, width), BF16)],
        compiler_params=ROOM,
        cost_estimate=cost(4 * tokens * kvb * keep * size * size, 3 << 20),
        name="hidden",
    )(value_idx, x1, x2, w_value)


def reverse_bits(value, bits):
    out = 0
    for _ in range(bits):
        out, value = out * 2 + value % 2, value // 2
    return out


def tile_kernel(per, bits, starts, me, ok, h, g, *refs):
    arrived, outs, stack = refs[:-len(starts) - 1], refs[-len(starts) - 1:-1], refs[-1]
    tokens = g.shape[0]
    size = h.shape[1]
    keep = ok.shape[1]
    stack[:tokens] = g[...]
    at = 0
    for part in arrived:
        wide = part.shape[1]
        stack[tokens:, at:at + wide] = part[...]
        at += wide
    flip = me[0] * per
    for out, start in zip(outs, starts):
        for i in range(out.shape[0]):
            position = start + i
            tile = (reverse_bits(position // per, bits) * per + position % per) ^ flip
            c, j = tile // keep, lax.rem(tile, keep)
            term = lax.dot_general(h[c], block(stack, ok[c, j], size), NN, preferred_element_type=F32)
            out[i] = term.astype(out.dtype)


def tile_call(runs, me, output_idx, hidden, g, arrived, ranks):
    kvb, size, stacked = hidden.shape
    keep = output_idx.shape[1]
    total = kvb * keep
    count = sum(n for _, n, _ in runs)
    return pl.pallas_call(
        functools.partial(
            tile_kernel, total // ranks, ranks.bit_length() - 1, [start for start, _, _ in runs]
        ),
        out_shape=[pltpu.VMEM((n, size, size), kind) for _, n, kind in runs],
        in_specs=[SMEM, SMEM] + [VMEM] * (2 + len(arrived)),
        out_specs=[VMEM] * len(runs),
        scratch_shapes=[pltpu.VMEM((stacked, g.shape[1]), BF16)],
        compiler_params=ROOM,
        cost_estimate=cost(2 * stacked * count * size * size, 2 << 20),
        name="tiles",
    )(me, output_idx, hidden, g, *arrived)


def exchange(value, axis, bit):
    count = lax.axis_size(axis)
    return lax.ppermute(value, axis, [(i, i ^ bit) for i in range(count)])


def from_behind(value, axis, steps):
    count = lax.axis_size(axis)
    return lax.ppermute(value, axis, [(i, (i + steps) % count) for i in range(count)])


def per_device(x_first, x_second, grad_first, value_tiles, output_tiles, value_keep, output_keep):
    w_value, w_output = value_tiles[0], output_tiles[0]
    value_idx, output_idx = value_keep[0], output_keep[0]
    g = grad_first[0]
    width = g.shape[1]
    ranks = lax.axis_size("dp")
    me = lax.axis_index("dp").astype(jnp.int32).reshape(1)
    parts = 4
    first = first_call(g, w_value, w_output, value_idx, output_idx, [width // parts] * parts)
    arrived = [from_behind(p, "section", -1) for p in first]
    hidden = hidden_call(x_first[0], x_second[0], w_value, value_idx)
    run = w_value.shape[0] * w_value.shape[1] // 8
    at = {"kd": 0, "kc": 1, "kb": 2, "ka": 3, "sd": 4, "sc": 5, "sb": 6, "sa": 7}
    tiles = functools.partial(
        tile_call, me=me, output_idx=output_idx, hidden=hidden, g=g, arrived=arrived, ranks=ranks
    )
    spec = lambda *names: [(at[n] * run, run, BF16 if n[0] == "s" else F32) for n in names]
    sa, ka = tiles(spec("sa", "ka"))
    got_a = exchange(sa, "dp", 1)
    sc, sb, sd, kc, kb, kd = tiles(spec("sc", "sb", "sd", "kc", "kb", "kd"))
    got_b, got_c, got_d = (exchange(s, "dp", 1) for s in (sb, sc, sd))
    half = run // 2
    out_a = (ka + got_a.astype(F32)).astype(BF16)
    near = [exchange(out_a[i * half:(i + 1) * half], "dp", 2) for i in (0, 1)]
    near_b = exchange((kb + got_b.astype(F32)).astype(BF16), "dp", 2)
    far = []
    for i in (0, 1):
        s = slice(i * half, (i + 1) * half)
        out_c = (kc[s] + got_c[s].astype(F32) + near[i].astype(F32)).astype(BF16)
        if i == 0:
            near[1], out_c = lax.optimization_barrier((near[1], out_c))
        far.append(exchange(out_c, "dp", 4))
    second = second_call(arrived, w_value, w_output, value_idx, output_idx)
    staying = kd + got_d.astype(F32) + near_b.astype(F32)
    staying = staying + jnp.concatenate(far, axis=0).astype(F32)
    bit = 8
    while bit < ranks:
        half = staying.shape[0] // 2
        came = exchange(staying[half:].astype(BF16), "dp", bit)
        staying = staying[:half] + came.astype(F32)
        bit *= 2
    weight_grad = staying * (1.0 / (2.0 * ranks))
    return second[None], weight_grad[None]


def solution(mesh):
    in_specs = (
        P("section", "dp", None),
        P("section", "dp", None),
        P("section", "dp", None),
        P("section", None, None, None, None),
        P("section", None, None, None, None),
        P("section", None, None),
        P("section", None, None),
    )
    out_specs = (P("section", "dp", None), P("section", "dp", None, None))
    return jax.shard_map(
        per_device, mesh=mesh, in_specs=in_specs, out_specs=out_specs, check_vma=False
    )
```

```python
import functools

import jax
import jax.numpy as jnp
from jax import lax
from jax.experimental import pallas as pl
from jax.experimental.pallas import tpu as pltpu
from jax.sharding import PartitionSpec as P


F32 = jnp.float32
BF16 = jnp.bfloat16
NT = (((1,), (1,)), ((), ()))
NN = (((1,), (0,)), ((), ()))
VMEM = pl.BlockSpec(memory_space=pltpu.VMEM)
SMEM = pl.BlockSpec(memory_space=pltpu.SMEM)
HBM = pl.BlockSpec(memory_space=pl.ANY)
ROOM = pltpu.CompilerParams(vmem_limit_bytes=16 << 20)
FULL = pltpu.CompilerParams(vmem_limit_bytes=60 * 1024 * 1024)


def cost(flops, nbytes):
    return pl.CostEstimate(flops=flops, bytes_accessed=nbytes, transcendentals=0)


def block(ref, index, size):
    return ref[:, pl.ds(pl.multiple_of(index * size, size), size)]


def pairs(keep):
    return [(j, j + 1) for j in range(0, keep, 2)]


def hidden_grad(ok, g, o, c):
    keep, size = o.shape[1], o.shape[2]
    total = None
    for both in pairs(keep):
        left = jnp.concatenate([block(g, ok[c, j], size) for j in both], axis=1)
        right = jnp.concatenate([o[c, j] for j in both], axis=1)
        term = lax.dot_general(left, right, NT, preferred_element_type=F32)
        total = term if total is None else total + term
    return total.astype(BF16)


def add_back(vk, hidden, v, c, acc):
    keep, size = v.shape[1], v.shape[2]
    for both in pairs(keep):
        right = jnp.concatenate([v[c, j] for j in both], axis=0)
        term = lax.dot_general(hidden, right, NT, preferred_element_type=F32)
        for i, j in enumerate(both):
            cols = pl.ds(pl.multiple_of(vk[c, j] * size, size), size)
            acc[:, cols] = acc[:, cols] + term[:, i * size:(i + 1) * size]


def write_parts(acc, outs):
    at = 0
    for out in outs:
        wide = out.shape[1]
        out[...] = acc[:, at:at + wide].astype(BF16)
        at += wide


def first_kernel(vk_hbm, ok_hbm, g_hbm, o_hbm, v_hbm, *refs):
    outs, (g, o, v, acc, vk, ok, sem, w_sem) = refs[:-8], refs[-8:]
    kvb = o.shape[0]
    copy = pltpu.make_async_copy
    small = [copy(ok_hbm, ok, sem.at[0]), copy(g_hbm, g, sem.at[1]), copy(vk_hbm, vk, sem.at[2])]
    o_copies = [copy(o_hbm.at[c], o.at[c], w_sem.at[0, c]) for c in range(kvb)]
    v_copies = [copy(v_hbm.at[c], v.at[c], w_sem.at[1, c]) for c in range(kvb)]
    for each in small + o_copies + v_copies:
        each.start()
    small[0].wait()
    small[1].wait()
    acc[...] = g[...].astype(F32)
    hidden = []
    for c in range(kvb):
        o_copies[c].wait()
        hidden.append(hidden_grad(ok, g, o, c))
    small[2].wait()
    for c in range(kvb):
        v_copies[c].wait()
        add_back(vk, hidden[c], v, c, acc)
    write_parts(acc, outs)


def first_call(g, w_value, w_output, value_idx, output_idx, widths):
    tokens, width = g.shape
    kvb, keep, size, _ = w_value.shape
    return pl.pallas_call(
        first_kernel,
        out_shape=[pltpu.VMEM((tokens, w), BF16) for w in widths],
        in_specs=[HBM] * 5,
        out_specs=[VMEM] * len(widths),
        scratch_shapes=[
            pltpu.VMEM((tokens, width), BF16),
            pltpu.VMEM(w_output.shape, BF16),
            pltpu.VMEM(w_value.shape, BF16),
            pltpu.VMEM((tokens, width), F32),
            pltpu.SMEM(value_idx.shape, jnp.int32),
            pltpu.SMEM(output_idx.shape, jnp.int32),
            pltpu.SemaphoreType.DMA((3,)),
            pltpu.SemaphoreType.DMA((2, kvb)),
        ],
        cost_estimate=cost(4 * tokens * kvb * keep * size * size, 5 << 20),
        name="first",
    )(value_idx, output_idx, g, w_output, w_value)


def fetch(sources, targets, sem):
    copies = [pltpu.make_async_copy(a, b, sem.at[i]) for i, (a, b) in enumerate(zip(sources, targets))]
    for copy in copies:
        copy.start()
    return copies


def second_kernel(count, vk_hbm, ok_hbm, o_hbm, v_hbm, *refs):
    parts, (out, o, v, g, acc, vk, ok, sem) = refs[:count], refs[count:]
    kvb = o.shape[0]
    both = [r.at[c] for r in (o_hbm, v_hbm) for c in range(kvb)]
    into = [r.at[c] for r in (o, v) for c in range(kvb)]
    copies = fetch([ok_hbm, vk_hbm] + both, [ok, vk] + into, sem)
    at = 0
    for part in parts:
        wide = part.shape[1]
        g[:, at:at + wide] = part[...]
        acc[:, at:at + wide] = part[...].astype(F32)
        at += wide
    copies[0].wait()
    hidden = []
    for c in range(kvb):
        copies[2 + c].wait()
        hidden.append(hidden_grad(ok, g, o, c))
    copies[1].wait()
    for c in range(kvb):
        copies[2 + kvb + c].wait()
        add_back(vk, hidden[c], v, c, acc)
    out[...] = acc[...].astype(BF16)


def second_call(parts, w_value, w_output, value_idx, output_idx):
    tokens = parts[0].shape[0]
    width = sum(part.shape[1] for part in parts)
    kvb, keep, size, _ = w_value.shape
    return pl.pallas_call(
        functools.partial(second_kernel, len(parts)),
        out_shape=jax.ShapeDtypeStruct((tokens, width), BF16),
        in_specs=[HBM] * 4 + [VMEM] * len(parts),
        out_specs=VMEM,
        scratch_shapes=[
            pltpu.VMEM(w_output.shape, BF16),
            pltpu.VMEM(w_value.shape, BF16),
            pltpu.VMEM((tokens, width), BF16),
            pltpu.VMEM((tokens, width), F32),
            pltpu.SMEM(value_idx.shape, jnp.int32),
            pltpu.SMEM(output_idx.shape, jnp.int32),
            pltpu.SemaphoreType.DMA((2 + 2 * kvb,)),
        ],
        compiler_params=FULL,
        cost_estimate=cost(4 * tokens * kvb * keep * size * size, 5 << 20),
        name="second",
    )(value_idx, output_idx, w_output, w_value, *parts)


def hidden_kernel(vk, x1, x2, v_hbm, out, x, v, sem):
    tokens = x1.shape[0]
    kvb, keep, size, _ = v.shape
    copies = fetch(
        [x1, x2] + [v_hbm.at[c] for c in range(kvb)],
        [x.at[pl.ds(0, tokens)], x.at[pl.ds(tokens, tokens)]] + [v.at[c] for c in range(kvb)],
        sem,
    )
    copies[0].wait()
    copies[1].wait()
    for c in range(kvb):
        copies[2 + c].wait()
        total = None
        for both in pairs(keep):
            left = jnp.concatenate([block(x, vk[c, j], size) for j in both], axis=1)
            right = jnp.concatenate([v[c, j] for j in both], axis=0)
            term = lax.dot_general(left, right, NN, preferred_element_type=F32)
            total = term if total is None else total + term
        out[c] = total.astype(BF16).T


def hidden_call(x1, x2, w_value, value_idx):
    tokens, width = x1.shape
    kvb, keep, size, _ = w_value.shape
    return pl.pallas_call(
        hidden_kernel,
        out_shape=pltpu.VMEM((kvb, size, 2 * tokens), BF16),
        in_specs=[SMEM, HBM, HBM, HBM],
        out_specs=VMEM,
        scratch_shapes=[
            pltpu.VMEM((2 * tokens, width), BF16),
            pltpu.VMEM(w_value.shape, BF16),
            pltpu.SemaphoreType.DMA((2 + kvb,)),
        ],
        compiler_params=FULL,
        cost_estimate=cost(4 * tokens * kvb * keep * size * size, 3 << 20),
        name="hidden",
    )(value_idx, x1, x2, w_value)


def reverse_bits(value, bits):
    out = 0
    for _ in range(bits):
        out, value = out * 2 + value % 2, value // 2
    return out


def tile_kernel(per, bits, starts, me, ok, h, g, *refs):
    arrived, outs, stack = refs[:-len(starts) - 1], refs[-len(starts) - 1:-1], refs[-1]
    tokens = g.shape[0]
    size = h.shape[1]
    keep = ok.shape[1]
    stack[:tokens] = g[...]
    at = 0
    for part in arrived:
        wide = part.shape[1]
        stack[tokens:, at:at + wide] = part[...]
        at += wide
    flip = me[0] * per
    for out, start in zip(outs, starts):
        for i in range(out.shape[0]):
            position = start + i
            tile = (reverse_bits(position // per, bits) * per + position % per) ^ flip
            c, j = tile // keep, lax.rem(tile, keep)
            term = lax.dot_general(h[c], block(stack, ok[c, j], size), NN, preferred_element_type=F32)
            out[i] = term.astype(out.dtype)


def tile_call(runs, me, output_idx, hidden, g, arrived, ranks):
    kvb, size, stacked = hidden.shape
    keep = output_idx.shape[1]
    total = kvb * keep
    count = sum(n for _, n, _ in runs)
    return pl.pallas_call(
        functools.partial(
            tile_kernel, total // ranks, ranks.bit_length() - 1, [start for start, _, _ in runs]
        ),
        out_shape=[pltpu.VMEM((n, size, size), kind) for _, n, kind in runs],
        in_specs=[SMEM, SMEM] + [VMEM] * (2 + len(arrived)),
        out_specs=[VMEM] * len(runs),
        scratch_shapes=[pltpu.VMEM((stacked, g.shape[1]), BF16)],
        compiler_params=ROOM,
        cost_estimate=cost(2 * stacked * count * size * size, 2 << 20),
        name="tiles",
    )(me, output_idx, hidden, g, *arrived)


def exchange(value, axis, bit):
    count = lax.axis_size(axis)
    return lax.ppermute(value, axis, [(i, i ^ bit) for i in range(count)])


def from_behind(value, axis, steps):
    count = lax.axis_size(axis)
    return lax.ppermute(value, axis, [(i, (i + steps) % count) for i in range(count)])


def per_device(x_first, x_second, grad_first, value_tiles, output_tiles, value_keep, output_keep):
    w_value, w_output = value_tiles[0], output_tiles[0]
    value_idx, output_idx = value_keep[0], output_keep[0]
    g = grad_first[0]
    width = g.shape[1]
    ranks = lax.axis_size("dp")
    me = lax.axis_index("dp").astype(jnp.int32).reshape(1)
    parts = 4
    first = first_call(g, w_value, w_output, value_idx, output_idx, [width // parts] * parts)
    arrived = [from_behind(p, "section", -1) for p in first]
    hidden = hidden_call(x_first[0], x_second[0], w_value, value_idx)
    run = w_value.shape[0] * w_value.shape[1] // 8
    at = {"kd": 0, "kc": 1, "kb": 2, "ka": 3, "sd": 4, "sc": 5, "sb": 6, "sa": 7}
    tiles = functools.partial(
        tile_call, me=me, output_idx=output_idx, hidden=hidden, g=g, arrived=arrived, ranks=ranks
    )
    spec = lambda *names: [(at[n] * run, run, BF16 if n[0] == "s" else F32) for n in names]
    sa, ka = tiles(spec("sa", "ka"))
    got_a = exchange(sa, "dp", 1)
    sc, sb, sd, kc, kb, kd = tiles(spec("sc", "sb", "sd", "kc", "kb", "kd"))
    got_b, got_c, got_d = (exchange(s, "dp", 1) for s in (sb, sc, sd))
    cuts = [slice(0, run // 4), slice(run // 4, run)]
    out_a = (ka + got_a.astype(F32)).astype(BF16)
    near = []
    for cut in cuts:
        near.append(exchange(out_a[cut], "dp", 2))
    near_b = exchange((kb + got_b.astype(F32)).astype(BF16), "dp", 2)
    far = []
    for i, cut in enumerate(cuts):
        out_c = (kc[cut] + got_c[cut].astype(F32) + near[i].astype(F32)).astype(BF16)
        if i == 0:
            near[1], _ = lax.optimization_barrier((near[1], out_c))
        far.append(exchange(out_c, "dp", 4))
    second = second_call(arrived, w_value, w_output, value_idx, output_idx)
    staying = kd + got_d.astype(F32) + near_b.astype(F32)
    staying, far = lax.optimization_barrier((staying, far))
    staying = staying + jnp.concatenate(far, axis=0).astype(F32)
    bit = 8
    while bit < ranks:
        half = staying.shape[0] // 2
        came = exchange(staying[half:].astype(BF16), "dp", bit)
        staying = staying[:half] + came.astype(F32)
        bit *= 2
    weight_grad = staying * (1.0 / (2.0 * ranks))
    return second[None], weight_grad[None]


def solution(mesh):
    in_specs = (
        P("section", "dp", None),
        P("section", "dp", None),
        P("section", "dp", None),
        P("section", None, None, None, None),
        P("section", None, None, None, None),
        P("section", None, None),
        P("section", None, None),
    )
    out_specs = (P("section", "dp", None), P("section", "dp", None, None))

    return jax.shard_map(
        per_device, mesh=mesh, in_specs=in_specs, out_specs=out_specs, check_vma=False
    )
```

```python
import functools

import jax
import jax.numpy as jnp
from jax import lax
from jax.experimental import pallas as pl
from jax.experimental.pallas import tpu as pltpu
from jax.sharding import PartitionSpec as P


F32 = jnp.float32
BF16 = jnp.bfloat16
NT = (((1,), (1,)), ((), ()))
NN = (((1,), (0,)), ((), ()))
VMEM = pl.BlockSpec(memory_space=pltpu.VMEM)
SMEM = pl.BlockSpec(memory_space=pltpu.SMEM)
HBM = pl.BlockSpec(memory_space=pl.ANY)
ROOM = pltpu.CompilerParams(vmem_limit_bytes=16 << 20)
FULL = pltpu.CompilerParams(vmem_limit_bytes=60 * 1024 * 1024)


def cost(flops, nbytes):
    return pl.CostEstimate(flops=flops, bytes_accessed=nbytes, transcendentals=0)


def block(ref, index, size):
    return ref[:, pl.ds(pl.multiple_of(index * size, size), size)]


def pairs(keep):
    return [(j, j + 1) for j in range(0, keep, 2)]


def hidden_grad(ok, g, o, c):
    keep, size = o.shape[1], o.shape[2]
    total = None
    for both in pairs(keep):
        left = jnp.concatenate([block(g, ok[c, j], size) for j in both], axis=1)
        right = jnp.concatenate([o[c, j] for j in both], axis=1)
        term = lax.dot_general(left, right, NT, preferred_element_type=F32)
        total = term if total is None else total + term
    return total.astype(BF16)


def add_back(vk, hidden, v, c, acc, first=0):
    keep, size = v.shape[1], v.shape[2]
    for both in pairs(keep):
        right = jnp.concatenate([v[c, j] for j in both], axis=0)
        term = lax.dot_general(hidden, right, NT, preferred_element_type=F32)
        for i, j in enumerate(both):
            cols = pl.ds(pl.multiple_of(vk[c, first + j] * size, size), size)
            acc[:, cols] = acc[:, cols] + term[:, i * size:(i + 1) * size]


def first_kernel(vk_hbm, ok_hbm, g_hbm, o_hbm, v_hbm, *refs):
    (chunk, acc, hidden, v_high, vk), (g, o, v_low, ok, sem, w_sem) = refs[:5], refs[5:]
    kvb, low, keep = o.shape[0], v_low.shape[1], v_hbm.shape[1]
    copy = pltpu.make_async_copy
    small = [copy(ok_hbm, ok, sem.at[0]), copy(g_hbm, g, sem.at[1]), copy(vk_hbm, vk, sem.at[2])]
    o_copies = [copy(o_hbm.at[c], o.at[c], w_sem.at[0, c]) for c in range(kvb)]
    v_copies = [copy(v_hbm.at[c, pl.ds(0, low)], v_low.at[c], w_sem.at[1, c]) for c in range(kvb)]
    rest = [copy(v_hbm.at[c, pl.ds(low, keep - low)], v_high.at[c], w_sem.at[2, c]) for c in range(kvb)]
    for each in small + o_copies:
        each.start()
    small[0].wait()
    small[1].wait()
    acc[...] = g[...].astype(F32)
    for c in range(kvb):
        o_copies[c].wait()
        v_copies[c].start()
        if c == kvb - 1:
            for each in rest:
                each.start()
        hidden[c] = hidden_grad(ok, g, o, c)
    small[2].wait()
    for c in range(kvb):
        v_copies[c].wait()
        add_back(vk, hidden[c], v_low, c, acc)
    chunk[...] = acc[:, :chunk.shape[1]].astype(BF16)
    for each in rest:
        each.wait()


def first_call(g, w_value, w_output, value_idx, output_idx, wide):
    tokens, width = g.shape
    kvb, keep, size, _ = w_value.shape
    low = wide // size
    return pl.pallas_call(
        first_kernel,
        out_shape=[
            pltpu.VMEM((tokens, wide), BF16),
            pltpu.VMEM((tokens, width), F32),
            pltpu.VMEM((kvb, tokens, size), BF16),
            pltpu.VMEM((kvb, keep - low, size, size), BF16),
            pltpu.SMEM(value_idx.shape, jnp.int32),
        ],
        in_specs=[HBM] * 5,
        out_specs=[VMEM] * 4 + [SMEM],
        scratch_shapes=[
            pltpu.VMEM((tokens, width), BF16),
            pltpu.VMEM(w_output.shape, BF16),
            pltpu.VMEM((kvb, low, size, size), BF16),
            pltpu.SMEM(output_idx.shape, jnp.int32),
            pltpu.SemaphoreType.DMA((3,)),
            pltpu.SemaphoreType.DMA((3, kvb)),
        ],
        compiler_params=FULL,
        cost_estimate=cost(3 * tokens * kvb * keep * size * size, 5 << 20),
        name="first",
    )(value_idx, output_idx, g, w_output, w_value)


def rest_kernel(vk, hidden, v_high, acc_in, acc, *outs):
    kvb, high = v_high.shape[0], v_high.shape[1]
    for c in range(kvb):
        add_back(vk, hidden[c], v_high, c, acc, vk.shape[1] - high)
    at = acc.shape[1] - sum(out.shape[1] for out in outs)
    for out in outs:
        wide = out.shape[1]
        out[...] = acc[:, at:at + wide].astype(BF16)
        at += wide


def rest_call(value_idx, hidden, v_high, acc, widths):
    tokens = acc.shape[0]
    return pl.pallas_call(
        rest_kernel,
        out_shape=[pltpu.VMEM(acc.shape, F32)] + [pltpu.VMEM((tokens, w), BF16) for w in widths],
        in_specs=[SMEM] + [VMEM] * 3,
        out_specs=[VMEM] * (1 + len(widths)),
        input_output_aliases={3: 0},
        compiler_params=ROOM,
        cost_estimate=cost(2 * tokens * v_high.size, 2 << 20),
        name="rest",
    )(value_idx, hidden, v_high, acc)[1:]


def fetch(sources, targets, sem):
    copies = [pltpu.make_async_copy(a, b, sem.at[i]) for i, (a, b) in enumerate(zip(sources, targets))]
    for copy in copies:
        copy.start()
    return copies


def second_kernel(vk_hbm, ok_hbm, o_hbm, v_hbm, stack, out, o, v, acc, vk, ok, sem):
    kvb = o.shape[0]
    both = [r.at[c] for r in (o_hbm, v_hbm) for c in range(kvb)]
    into = [r.at[c] for r in (o, v) for c in range(kvb)]
    copies = fetch([ok_hbm, vk_hbm] + both, [ok, vk] + into, sem)
    tokens = acc.shape[0]
    g = stack.at[pl.ds(tokens, tokens)]
    acc[...] = g[...].astype(F32)
    copies[0].wait()
    hidden = []
    for c in range(kvb):
        copies[2 + c].wait()
        hidden.append(hidden_grad(ok, g, o, c))
    copies[1].wait()
    for c in range(kvb):
        copies[2 + kvb + c].wait()
        add_back(vk, hidden[c], v, c, acc)
    out[...] = acc[...].astype(BF16)


def second_call(stack, w_value, w_output, value_idx, output_idx):
    tokens, width = stack.shape[0] // 2, stack.shape[1]
    kvb, keep, size, _ = w_value.shape
    return pl.pallas_call(
        second_kernel,
        out_shape=jax.ShapeDtypeStruct((tokens, width), BF16),
        in_specs=[HBM] * 4 + [VMEM],
        out_specs=VMEM,
        scratch_shapes=[
            pltpu.VMEM(w_output.shape, BF16),
            pltpu.VMEM(w_value.shape, BF16),
            pltpu.VMEM((tokens, width), F32),
            pltpu.SMEM(value_idx.shape, jnp.int32),
            pltpu.SMEM(output_idx.shape, jnp.int32),
            pltpu.SemaphoreType.DMA((2 + 2 * kvb,)),
        ],
        compiler_params=FULL,
        cost_estimate=cost(4 * tokens * kvb * keep * size * size, 5 << 20),
        name="second",
    )(value_idx, output_idx, w_output, w_value, stack)


def hidden_kernel(vk, x1, x2, v_hbm, out, x, v, sem):
    tokens = x1.shape[0]
    kvb, keep, size, _ = v.shape
    copies = fetch(
        [x1, x2] + [v_hbm.at[c] for c in range(kvb)],
        [x.at[pl.ds(0, tokens)], x.at[pl.ds(tokens, tokens)]] + [v.at[c] for c in range(kvb)],
        sem,
    )
    copies[0].wait()
    copies[1].wait()
    for c in range(kvb):
        copies[2 + c].wait()
        total = None
        for both in pairs(keep):
            left = jnp.concatenate([block(x, vk[c, j], size) for j in both], axis=1)
            right = jnp.concatenate([v[c, j] for j in both], axis=0)
            term = lax.dot_general(left, right, NN, preferred_element_type=F32)
            total = term if total is None else total + term
        out[c] = total.astype(BF16).T


def hidden_call(x1, x2, w_value, value_idx):
    tokens, width = x1.shape
    kvb, keep, size, _ = w_value.shape
    return pl.pallas_call(
        hidden_kernel,
        out_shape=pltpu.VMEM((kvb, size, 2 * tokens), BF16),
        in_specs=[SMEM, HBM, HBM, HBM],
        out_specs=VMEM,
        scratch_shapes=[
            pltpu.VMEM((2 * tokens, width), BF16),
            pltpu.VMEM(w_value.shape, BF16),
            pltpu.SemaphoreType.DMA((2 + kvb,)),
        ],
        compiler_params=FULL,
        cost_estimate=cost(4 * tokens * kvb * keep * size * size, 3 << 20),
        name="hidden",
    )(value_idx, x1, x2, w_value)


def reverse_bits(value, bits):
    out = 0
    for _ in range(bits):
        out, value = out * 2 + value % 2, value // 2
    return out


def stack_kernel(ok, me, g, *refs):
    parts, (stack, ok_out, me_out) = refs[:-3], refs[-3:]
    me_out[0] = me[0]
    for c in range(ok.shape[0]):
        for j in range(ok.shape[1]):
            ok_out[c, j] = ok[c, j]
    tokens = g.shape[0]
    stack[:tokens] = g[...]
    at = 0
    for part in parts:
        wide = part.shape[1]
        stack[tokens:, at:at + wide] = part[...]
        at += wide


def stack_call(output_idx, me, g, parts):
    tokens, width = g.shape
    return pl.pallas_call(
        stack_kernel,
        out_shape=[
            pltpu.VMEM((2 * tokens, width), BF16),
            pltpu.SMEM(output_idx.shape, jnp.int32),
            pltpu.SMEM(me.shape, jnp.int32),
        ],
        in_specs=[SMEM, SMEM] + [VMEM] * (1 + len(parts)),
        out_specs=[VMEM, SMEM, SMEM],
        compiler_params=ROOM,
        cost_estimate=cost(0, 1 << 20),
        name="stack",
    )(output_idx, me, g, *parts)


def tile_kernel(per, bits, starts, me, ok, h, stack, *refs):
    outs = refs[-len(starts):]
    size = h.shape[1]
    keep = ok.shape[1]
    if len(refs) > len(starts):
        part, stack = refs[0], refs[1]
        tokens, wide = part.shape
        stack[tokens:, stack.shape[1] - wide:] = part[...]
    flip = me[0] * per
    for out, start in zip(outs, starts):
        for i in range(out.shape[0]):
            position = start + i
            tile = (reverse_bits(position // per, bits) * per + position % per) ^ flip
            c, j = tile // keep, lax.rem(tile, keep)
            term = lax.dot_general(h[c], block(stack, ok[c, j], size), NN, preferred_element_type=F32)
            out[i] = term.astype(out.dtype)


def tile_call(runs, me, output_idx, hidden, stack, ranks, part=()):
    kvb, size, stacked = hidden.shape
    keep = output_idx.shape[1]
    total = kvb * keep
    count = sum(n for _, n, _ in runs)
    outs = [pltpu.VMEM((n, size, size), kind) for _, n, kind in runs]
    if part:
        outs = [pltpu.VMEM(stack.shape, BF16)] + outs
    return pl.pallas_call(
        functools.partial(
            tile_kernel, total // ranks, ranks.bit_length() - 1, [start for start, _, _ in runs]
        ),
        out_shape=outs,
        in_specs=[SMEM, SMEM] + [VMEM] * (2 + len(part)),
        out_specs=[VMEM] * len(outs),
        input_output_aliases={3: 0} if part else {},
        compiler_params=ROOM,
        cost_estimate=cost(2 * stacked * count * size * size, 2 << 20),
        name="tiles",
    )(me, output_idx, hidden, stack, *part)


def exchange(value, axis, bit):
    count = lax.axis_size(axis)
    return lax.ppermute(value, axis, [(i, i ^ bit) for i in range(count)])


def from_behind(value, axis, steps):
    count = lax.axis_size(axis)
    return lax.ppermute(value, axis, [(i, (i + steps) % count) for i in range(count)])


def per_device(x_first, x_second, grad_first, value_tiles, output_tiles, value_keep, output_keep):
    w_value, w_output = value_tiles[0], output_tiles[0]
    value_idx, output_idx = value_keep[0], output_keep[0]
    g = grad_first[0]
    width = g.shape[1]
    ranks = lax.axis_size("dp")
    me = lax.axis_index("dp").astype(jnp.int32).reshape(1)
    parts = 4
    wide = width // parts
    chunk, acc, down, v_high, vk = first_call(g, w_value, w_output, value_idx, output_idx, wide)
    arrived = [from_behind(chunk, "section", -1)]
    others = rest_call(vk, down, v_high, acc, [wide] * (parts - 1))
    for part in others:
        arrived.append(from_behind(part, "section", -1))
    hidden = hidden_call(x_first[0], x_second[0], w_value, value_idx)
    run = w_value.shape[0] * w_value.shape[1] // 8
    at = {"kd": 0, "kc": 1, "kb": 2, "ka": 3, "sd": 4, "sc": 5, "sb": 6, "sa": 7}
    stack, kept_idx, me = stack_call(output_idx, me, g, arrived[:-1])
    tiles = functools.partial(
        tile_call, me=me, output_idx=kept_idx, hidden=hidden, ranks=ranks
    )
    spec = lambda *names: [(at[n] * run, run, BF16 if n[0] == "s" else F32) for n in names]
    few = run // 4
    first_tiles = [(at["sa"] * run, few, BF16), (at["sa"] * run + few, run - few, BF16)]
    stack, sa0, sa1, ka = tiles(first_tiles + spec("ka"), stack=stack, part=arrived[-1:])
    got_a = []
    for part in (sa0, sa1):
        got_a.append(exchange(part, "dp", 1))
    sc, kc = tiles(spec("sc", "kc"), stack=stack)
    got_c = exchange(sc, "dp", 1)
    sb, sd, kb, kd = tiles(spec("sb", "sd", "kb", "kd"), stack=stack)
    got_b, got_d = (exchange(s, "dp", 1) for s in (sb, sd))
    cuts = [slice(0, few), slice(few, run)]
    near = []
    for i, cut in enumerate(cuts):
        near.append(exchange((ka[cut] + got_a[i].astype(F32)).astype(BF16), "dp", 2))
        if i == 0:
            got_a[1], _ = lax.optimization_barrier((got_a[1], got_a[0]))
    near_b = exchange((kb + got_b.astype(F32)).astype(BF16), "dp", 2)
    far = []
    for i, cut in enumerate(cuts):
        out_c = (kc[cut] + got_c[cut].astype(F32) + near[i].astype(F32)).astype(BF16)
        if i == 0:
            near[1], _ = lax.optimization_barrier((near[1], out_c))
        far.append(exchange(out_c, "dp", 4))
    second = second_call(stack, w_value, w_output, value_idx, output_idx)
    staying = kd + got_d.astype(F32) + near_b.astype(F32)
    staying, far = lax.optimization_barrier((staying, far))
    staying = staying + jnp.concatenate(far, axis=0).astype(F32)
    bit = 8
    while bit < ranks:
        half = staying.shape[0] // 2
        came = exchange(staying[half:].astype(BF16), "dp", bit)
        staying = staying[:half] + came.astype(F32)
        bit *= 2
    weight_grad = staying * (1.0 / (2.0 * ranks))
    return second[None], weight_grad[None]


def solution(mesh):
    in_specs = (
        P("section", "dp", None),
        P("section", "dp", None),
        P("section", "dp", None),
        P("section", None, None, None, None),
        P("section", None, None, None, None),
        P("section", None, None),
        P("section", None, None),
    )
    out_specs = (P("section", "dp", None), P("section", "dp", None, None))

    return jax.shard_map(
        per_device, mesh=mesh, in_specs=in_specs, out_specs=out_specs, check_vma=False
    )
```

```python
import functools

import jax
import jax.numpy as jnp
from jax import lax
from jax.experimental import pallas as pl
from jax.experimental.pallas import tpu as pltpu
from jax.sharding import PartitionSpec as P


F32 = jnp.float32
BF16 = jnp.bfloat16
NT = (((1,), (1,)), ((), ()))
NN = (((1,), (0,)), ((), ()))
VMEM = pl.BlockSpec(memory_space=pltpu.VMEM)
SMEM = pl.BlockSpec(memory_space=pltpu.SMEM)
HBM = pl.BlockSpec(memory_space=pl.ANY)
ROOM = pltpu.CompilerParams(vmem_limit_bytes=16 << 20)
FULL = pltpu.CompilerParams(vmem_limit_bytes=60 * 1024 * 1024)


def cost(flops, nbytes):
    return pl.CostEstimate(flops=flops, bytes_accessed=nbytes, transcendentals=0)


def block(ref, index, size):
    return ref[:, pl.ds(pl.multiple_of(index * size, size), size)]


def pairs(keep):
    return [(j, j + 1) for j in range(0, keep, 2)]


def hidden_grad(ok, g, o, c, place=lambda index: index):
    keep, size = o.shape[1], o.shape[2]
    total = None
    for both in pairs(keep):
        left = jnp.concatenate([block(g, place(ok[c, j]), size) for j in both], axis=1)
        right = jnp.concatenate([o[c, j] for j in both], axis=1)
        term = lax.dot_general(left, right, NT, preferred_element_type=F32)
        total = term if total is None else total + term
    return total.astype(BF16)


def add_back(vk, hidden, v, c, acc):
    keep, size = v.shape[1], v.shape[2]
    for both in pairs(keep):
        right = jnp.concatenate([v[c, j] for j in both], axis=0)
        term = lax.dot_general(hidden, right, NT, preferred_element_type=F32)
        for i, j in enumerate(both):
            cols = pl.ds(pl.multiple_of(vk[c, j] * size, size), size)
            acc[:, cols] = acc[:, cols] + term[:, i * size:(i + 1) * size]


def kept_before(row, keep, blocks):
    count = jnp.int32(0)
    for b in range(blocks):
        kept = jnp.logical_and(count < keep, row(jnp.minimum(count, keep - 1)) == b)
        yield b, kept, count
        count = count + kept.astype(jnp.int32)


def urgent_row(me, kvb):
    return lax.rem((me[0] // 2) ^ (kvb - 1), kvb)


def down_kernel(vk_hbm, ok_hbm, me_hbm, g_hbm, o_hbm, v_hbm, hidden, g, v, vk, ok, me, o, sem, w_sem):
    kvb = o.shape[0]
    copy = pltpu.make_async_copy
    small = [copy(ok_hbm, ok, sem.at[0]), copy(g_hbm, g, sem.at[1])]
    small += [copy(vk_hbm, vk, sem.at[2]), copy(me_hbm, me, sem.at[3])]
    o_copies = [copy(o_hbm.at[c], o.at[c], w_sem.at[0, c]) for c in range(kvb)]
    v_copies = [copy(v_hbm.at[c], v.at[c], w_sem.at[1, c]) for c in range(kvb)]

    def start(copies):
        for each in copies:
            each.start()

    start(small + o_copies[:2])
    small[0].wait()
    start(o_copies[2:])
    small[1].wait()
    start(v_copies)
    for c in range(kvb):
        o_copies[c].wait()
        hidden[c] = hidden_grad(ok, g, o, c)
    for each in small[2:] + v_copies:
        each.wait()


def down_call(me, g, w_value, w_output, value_idx, output_idx):
    tokens, width = g.shape
    kvb, keep, size, _ = w_value.shape
    return pl.pallas_call(
        down_kernel,
        out_shape=[
            pltpu.VMEM((kvb, tokens, size), BF16),
            pltpu.VMEM((tokens, width), BF16),
            pltpu.VMEM(w_value.shape, BF16),
            pltpu.SMEM(value_idx.shape, jnp.int32),
            pltpu.SMEM(output_idx.shape, jnp.int32),
            pltpu.SMEM(me.shape, jnp.int32),
        ],
        in_specs=[HBM] * 6,
        out_specs=[VMEM] * 3 + [SMEM] * 3,
        scratch_shapes=[
            pltpu.VMEM(w_output.shape, BF16),
            pltpu.SemaphoreType.DMA((4,)),
            pltpu.SemaphoreType.DMA((2, kvb)),
        ],
        compiler_params=FULL,
        cost_estimate=cost(2 * tokens * kvb * keep * size * size, 5 << 20),
        name="down",
    )(value_idx, output_idx, me, g, w_output, w_value)


def up_kernel(vk, me, theirs_hbm, hidden, g, v, half, whole, theirs, acc, sem):
    kvb, keep, size, _ = v.shape
    copy = pltpu.make_async_copy(theirs_hbm, theirs, sem.at[0])
    copy.start()
    acc[...] = g[...].astype(F32)
    for c in range(kvb):
        add_back(vk, hidden[c], v, c, acc)
    copy.wait()
    row = urgent_row(me, kvb)
    for i in range(keep):
        half[:, i * size:(i + 1) * size] = block(acc, theirs[row, i], size).astype(BF16)
    whole[...] = acc[...].astype(BF16)


def up_call(value_idx, me, theirs, hidden, g, v):
    tokens, width = g.shape
    _, keep, size, _ = v.shape
    return pl.pallas_call(
        up_kernel,
        out_shape=[
            pltpu.VMEM((tokens, keep * size), BF16),
            pltpu.VMEM((tokens, width), BF16),
            pltpu.SMEM(theirs.shape, jnp.int32),
        ],
        in_specs=[SMEM, SMEM, HBM, VMEM, VMEM, VMEM],
        out_specs=[VMEM, VMEM, SMEM],
        scratch_shapes=[pltpu.VMEM((tokens, width), F32), pltpu.SemaphoreType.DMA((1,))],
        compiler_params=ROOM,
        cost_estimate=cost(2 * tokens * v.size, 2 << 20),
        name="up",
    )(value_idx, me, theirs, hidden, g, v)


def pack_kernel(theirs, me, whole, out, wide):
    width = whole.shape[1]
    kvb, keep = theirs.shape
    size = (wide.shape[1] - out.shape[1])
    blocks = width // size
    row = urgent_row(me, kvb)
    for b, kept, count in kept_before(lambda i: theirs[row, i], keep, blocks):
        at = jnp.where(kept, blocks - keep, b - count)
        cols = pl.ds(pl.multiple_of(at * size, size), size)
        wide[:, cols] = whole[:, b * size:(b + 1) * size]
    out[...] = wide[:, :out.shape[1]]


def pack_call(theirs, me, whole, size):
    tokens, width = whole.shape
    rest = width - theirs.shape[1] * size
    return pl.pallas_call(
        pack_kernel,
        out_shape=pltpu.VMEM((tokens, rest), BF16),
        in_specs=[SMEM, SMEM, VMEM],
        out_specs=VMEM,
        scratch_shapes=[pltpu.VMEM((tokens, rest + size), BF16)],
        compiler_params=ROOM,
        cost_estimate=cost(0, 1 << 20),
        name="pack",
    )(theirs, me, whole)


def fetch(sources, targets, sem):
    copies = [pltpu.make_async_copy(a, b, sem.at[i]) for i, (a, b) in enumerate(zip(sources, targets))]
    for copy in copies:
        copy.start()
    return copies


def second_kernel(vk, ok, spot, o_hbm, v_hbm, stack, out, o, v, acc, sem):
    kvb, size = o.shape[0], o.shape[2]
    both = [r.at[c] for r in (o_hbm, v_hbm) for c in range(kvb)]
    into = [r.at[c] for r in (o, v) for c in range(kvb)]
    copies = fetch(both, into, sem)
    tokens = acc.shape[0]
    g = stack.at[pl.ds(tokens, tokens)]
    for b in range(acc.shape[1] // size):
        acc[:, b * size:(b + 1) * size] = block(g, spot[b], size).astype(F32)
    hidden = []
    for c in range(kvb):
        copies[c].wait()
        hidden.append(hidden_grad(ok, g, o, c, lambda index: spot[index]))
    for c in range(kvb):
        copies[kvb + c].wait()
        add_back(vk, hidden[c], v, c, acc)
    out[...] = acc[...].astype(BF16)


def second_call(stack, w_value, w_output, value_idx, output_idx, spot):
    tokens, width = stack.shape[0] // 2, stack.shape[1]
    kvb, keep, size, _ = w_value.shape
    return pl.pallas_call(
        second_kernel,
        out_shape=jax.ShapeDtypeStruct((tokens, width), BF16),
        in_specs=[SMEM] * 3 + [HBM] * 2 + [VMEM],
        out_specs=VMEM,
        scratch_shapes=[
            pltpu.VMEM(w_output.shape, BF16),
            pltpu.VMEM(w_value.shape, BF16),
            pltpu.VMEM((tokens, width), F32),
            pltpu.SemaphoreType.DMA((2 * kvb,)),
        ],
        compiler_params=FULL,
        cost_estimate=cost(4 * tokens * kvb * keep * size * size, 5 << 20),
        name="second",
    )(value_idx, output_idx, spot, w_output, w_value, stack)


def hidden_kernel(vk, x1, x2, v_hbm, out, x, v, sem):
    tokens = x1.shape[0]
    kvb, keep, size, _ = v.shape
    copies = fetch(
        [x1, x2] + [v_hbm.at[c] for c in range(kvb)],
        [x.at[pl.ds(0, tokens)], x.at[pl.ds(tokens, tokens)]] + [v.at[c] for c in range(kvb)],
        sem,
    )
    copies[0].wait()
    copies[1].wait()
    for c in range(kvb):
        copies[2 + c].wait()
        total = None
        for both in pairs(keep):
            left = jnp.concatenate([block(x, vk[c, j], size) for j in both], axis=1)
            right = jnp.concatenate([v[c, j] for j in both], axis=0)
            term = lax.dot_general(left, right, NN, preferred_element_type=F32)
            total = term if total is None else total + term
        out[c] = total.astype(BF16).T


def hidden_call(x1, x2, w_value, value_idx):
    tokens, width = x1.shape
    kvb, keep, size, _ = w_value.shape
    return pl.pallas_call(
        hidden_kernel,
        out_shape=pltpu.VMEM((kvb, size, 2 * tokens), BF16),
        in_specs=[SMEM, HBM, HBM, HBM],
        out_specs=VMEM,
        scratch_shapes=[
            pltpu.VMEM((2 * tokens, width), BF16),
            pltpu.VMEM(w_value.shape, BF16),
            pltpu.SemaphoreType.DMA((2 + kvb,)),
        ],
        compiler_params=FULL,
        cost_estimate=cost(4 * tokens * kvb * keep * size * size, 3 << 20),
        name="hidden",
    )(value_idx, x1, x2, w_value)


def reverse_bits(value, bits):
    out = 0
    for _ in range(bits):
        out, value = out * 2 + value % 2, value // 2
    return out


def stack_kernel(ok, me, g, stack, spot):
    tokens, width = g.shape
    kvb, keep = ok.shape
    blocks = spot.shape[0]
    size = width // blocks
    row = urgent_row(me, kvb)
    for b, kept, count in kept_before(lambda i: ok[row, i], keep, blocks):
        at = jnp.where(kept, count, keep + b - count)
        spot[b] = at
        cols = pl.ds(pl.multiple_of(at * size, size), size)
        stack[:tokens, cols] = g[:, b * size:(b + 1) * size]


def stack_call(output_idx, me, g, size):
    tokens, width = g.shape
    return pl.pallas_call(
        stack_kernel,
        out_shape=[pltpu.VMEM((2 * tokens, width), BF16), pltpu.SMEM((width // size,), jnp.int32)],
        in_specs=[SMEM, SMEM, VMEM],
        out_specs=[VMEM, SMEM],
        compiler_params=ROOM,
        cost_estimate=cost(0, 1 << 20),
        name="stack",
    )(output_idx, me, g)


def tile_kernel(per, bits, starts, offsets, me, ok, spot, h, stack, *refs):
    outs = refs[-len(starts):]
    size = h.shape[1]
    keep = ok.shape[1]
    if offsets:
        stack = refs[len(offsets)]
        for part, at in zip(refs, offsets):
            tokens, wide = part.shape
            stack[tokens:, at:at + wide] = part[...]
    flip = me[0] * per
    for out, start in zip(outs, starts):
        for i in range(out.shape[0]):
            position = start + i
            tile = (reverse_bits(position // per, bits) * per + position % per) ^ flip
            c, j = tile // keep, lax.rem(tile, keep)
            right = block(stack, spot[ok[c, j]], size)
            term = lax.dot_general(h[c], right, NN, preferred_element_type=F32)
            out[i] = term.astype(out.dtype)


def tile_call(runs, me, output_idx, spot, hidden, stack, ranks, parts=()):
    kvb, size, stacked = hidden.shape
    keep = output_idx.shape[1]
    total = kvb * keep
    count = sum(n for _, n, _ in runs)
    outs = [pltpu.VMEM((n, size, size), kind) for _, n, kind in runs]
    if parts:
        outs = [pltpu.VMEM(stack.shape, BF16)] + outs
    starts, offsets = [start for start, _, _ in runs], [at for _, at in parts]
    return pl.pallas_call(
        functools.partial(tile_kernel, total // ranks, ranks.bit_length() - 1, starts, offsets),
        out_shape=outs,
        in_specs=[SMEM] * 3 + [VMEM] * (2 + len(parts)),
        out_specs=[VMEM] * len(outs),
        input_output_aliases={4: 0} if parts else {},
        compiler_params=ROOM,
        cost_estimate=cost(2 * stacked * count * size * size, 2 << 20),
        name="tiles",
    )(me, output_idx, spot, hidden, stack, *[part for part, _ in parts])


def exchange(value, axis, bit):
    count = lax.axis_size(axis)
    return lax.ppermute(value, axis, [(i, i ^ bit) for i in range(count)])


def from_behind(value, axis, steps):
    count = lax.axis_size(axis)
    return lax.ppermute(value, axis, [(i, (i + steps) % count) for i in range(count)])


def per_device(x_first, x_second, grad_first, value_tiles, output_tiles, value_keep, output_keep):
    w_value, w_output = value_tiles[0], output_tiles[0]
    value_idx, output_idx = value_keep[0], output_keep[0]
    g = grad_first[0]
    ranks = lax.axis_size("dp")
    me = lax.axis_index("dp").astype(jnp.int32).reshape(1)
    kvb, _, size, _ = w_value.shape
    theirs = from_behind(output_idx, "section", 1)
    down, g_here, v_here, vk, ok, me = down_call(me, g, w_value, w_output, value_idx, output_idx)
    half, whole, theirs = up_call(vk, me, theirs, down, g_here, v_here)
    arrived = [from_behind(half, "section", -1)]
    stack, spot = stack_call(ok, me, g_here, size)
    hidden = hidden_call(x_first[0], x_second[0], w_value, value_idx)
    whole, hidden, stack = lax.optimization_barrier((whole, hidden, stack))
    other = pack_call(theirs, me, whole, size)
    arrived.append(from_behind(other, "section", -1))
    parts = [(arrived[0], 0), (arrived[1], half.shape[1])]
    run = w_value.shape[0] * w_value.shape[1] // 8
    at = {"kd": 0, "kc": 1, "kb": 2, "ka": 3, "sd": 4, "sc": 5, "sb": 6, "sa": 7}
    tiles = functools.partial(
        tile_call, me=me, output_idx=ok, spot=spot, hidden=hidden, ranks=ranks
    )
    spec = lambda *names: [(at[n] * run, run, BF16 if n[0] == "s" else F32) for n in names]
    few = 3 * run // 8
    first_tiles = [(at["sa"] * run, few, BF16), (at["sa"] * run + few, run - few, BF16)]
    now = 1 if ranks == 2 * kvb else 2
    stack, sa0, sa1, ka = tiles(first_tiles + spec("ka"), stack=stack, parts=parts[:now])
    got_a = []
    for part in (sa0, sa1):
        got_a.append(exchange(part, "dp", 1))
    if parts[now:]:
        stack, sc, kc = tiles(spec("sc", "kc"), stack=stack, parts=parts[now:])
    else:
        sc, kc = tiles(spec("sc", "kc"), stack=stack)
    got_c = exchange(sc, "dp", 1)
    sb, sd, kb, kd = tiles(spec("sb", "sd", "kb", "kd"), stack=stack)
    got_b, got_d = (exchange(s, "dp", 1) for s in (sb, sd))
    cuts = [slice(0, few), slice(few, run)]
    near = []
    for i, cut in enumerate(cuts):
        out_a = (ka[cut] + got_a[i].astype(F32)).astype(BF16)
        if i == 0:
            got_a[1], _ = lax.optimization_barrier((got_a[1], out_a))
        near.append(exchange(out_a, "dp", 2))
    near_b = exchange((kb + got_b.astype(F32)).astype(BF16), "dp", 2)
    far = []
    for i, cut in enumerate(cuts):
        out_c = (kc[cut] + got_c[cut].astype(F32) + near[i].astype(F32)).astype(BF16)
        if i == 0:
            near[1], _ = lax.optimization_barrier((near[1], out_c))
        far.append(exchange(out_c, "dp", 4))
    second = second_call(stack, w_value, w_output, vk, ok, spot)
    staying = kd + got_d.astype(F32) + near_b.astype(F32)
    staying, far = lax.optimization_barrier((staying, far))
    staying = staying + jnp.concatenate(far, axis=0).astype(F32)
    bit = 8
    while bit < ranks:
        half = staying.shape[0] // 2
        came = exchange(staying[half:].astype(BF16), "dp", bit)
        staying = staying[:half] + came.astype(F32)
        bit *= 2
    weight_grad = staying * (1.0 / (2.0 * ranks))
    return second[None], weight_grad[None]


def solution(mesh):
    in_specs = (
        P("section", "dp", None),
        P("section", "dp", None),
        P("section", "dp", None),
        P("section", None, None, None, None),
        P("section", None, None, None, None),
        P("section", None, None),
        P("section", None, None),
    )
    out_specs = (P("section", "dp", None), P("section", "dp", None, None))

    return jax.shard_map(
        per_device, mesh=mesh, in_specs=in_specs, out_specs=out_specs, check_vma=False
    )
```
